512 devices in a mesh: vox: 8 (over z_lo), frm: 64 (over z_hi, y, x, core).
Axes of the slice: x: 4, y: 4, z: 16 (z_hi: 2, z_lo: 8; z = z_hi * 8 + z_lo), core: 2. Of those that a mesh axis runs over, the one named last changes fastest.
Arguments:
- spatial_coeffs: bfloat16 [2, 32, 256, 256], P(None, None, 'vox'), may hold values from -15 to 15
- temporal_basis: bfloat16 [32, 512], P(None, 'frm'), may hold values from -0.25 to 0.25
- coil_maps: bfloat16 [2, 4, 256, 256], P(None, None, 'vox'), may hold values from -4 to 4
- line_index: int32 [512, 8], P('frm'), may hold values from 0 to 255
- kspace_data: bfloat16 [512, 4, 2, 8, 256], P('frm', None, None, None, 'vox'), may hold values from -6 to 6
Outputs:
- coeff_grad: float32 [256, 2, 32, 256], P('frm', None, None, 'vox')
- basis_grad: float32 [32, 512], P(None, 'frm')
The draws below stay inside these ranges and needn't reach their ends.
Inputs may be any that keep to these rules, and one draw needn't show every extreme that they name: `line_index`: line numbers are drawn independently; a line may be sampled twice in one frame.
All inputs are finite; a program needn't handle non-finite values.
Results may differ from the reference program's by a relative error of at most 0.012.
Values may be sent and summed in bfloat16 or wider, within the bound.
No kernel may reach another device: no remote copies, remote signals or barrier semaphores. Data moves between devices by JAX's collectives and lax.ppermute only.
A program may use at most 64 MiB of HBM per device.

```python
import math
import jax
import jax.numpy as jnp
from jax import lax

NR = 256
NC = 256
L = 32
C = 4
K = 8
F_DEV = 8
FRAMES = 512


def place_ends(result, key, low, high):
    spot = [jax.random.randint(jax.random.fold_in(key, axis), (), 0, length) for axis, length in enumerate(result.shape)]
    widest = result.shape.index(max(result.shape))
    next_to = spot[:widest] + [(spot[widest] + 1) % result.shape[widest]] + spot[widest + 1:]
    return result.at[tuple(spot)].set(low).at[tuple(next_to)].set(high)


def block_levels(own_key, dims, pieces, smallest, top_value):
    def one(dim, shards_of):
        steps = jax.random.uniform(jax.random.fold_in(jax.random.fold_in(own_key, 6), dim), (shards_of,), jnp.float32, smallest / len(pieces), top_value / len(pieces))
        return jnp.repeat(jnp.exp(steps), dims[dim] // shards_of).reshape((-1,) + (1,) * (len(dims) - dim - 1))

    loudness = one(*pieces[0])
    for cut in pieces[1:]:
        loudness = loudness * one(*cut)
    return loudness


def centred(key, shape, width, most, shards=(), held_as=jnp.bfloat16):
    level = block_levels(key, shape, shards, -0.22, 0.18) if shards else 1.0
    entries = jax.random.normal(key, shape, jnp.float32) * width * level
    return jnp.minimum(jnp.maximum(entries, -most), most).astype(held_as)


def setup_inputs(seed: int = 0) -> dict:
    arg_keys = jax.random.split(jax.random.key(seed), 6)
    return {
        "spatial_coeffs": centred(arg_keys[0], (2, L, NR, NC), 3.0, 15.0, ((2, 8),)),
        "temporal_basis": centred(arg_keys[1], (L, FRAMES), FRAMES ** -0.5, 0.25, ((1, 64),)),
        "coil_maps": centred(arg_keys[2], (2, C, NR, NC), 0.7, 4.0, ((2, 8),)),
        "line_index": place_ends(jax.random.randint(arg_keys[3], (FRAMES, K), 0, NR), jax.random.fold_in(arg_keys[3], 1), 0, NR - 1).astype(jnp.int32),
        "kspace_data": centred(arg_keys[4], (FRAMES, C, 2, K, NC), 1.0, 6.0, ((0, 64), (4, 8))),
    }


def keep_bf16(values):
    return lax.optimization_barrier(values.astype(jnp.bfloat16)).astype(jnp.float32)

def dft_tables(length):
    indices = jnp.arange(length, dtype=jnp.int32)
    phases = indices[:, None] * indices[None, :] % length
    angles = phases.astype(jnp.float32) * (2.0 * math.pi / length)
    factor = 1.0 / math.sqrt(length)
    cosine = keep_bf16(jnp.cos(angles) * factor)
    sine = keep_bf16(-jnp.sin(angles) * factor)
    return (cosine, sine)

def line_tables(line_block, length):
    indices = jnp.arange(length, dtype=jnp.int32)
    phases = line_block[:, :, None] * indices[None, None, :] % length
    angles = phases.astype(jnp.float32) * (2.0 * math.pi / length)
    factor = 1.0 / math.sqrt(length)
    return (keep_bf16(jnp.cos(angles) * factor), keep_bf16(-jnp.sin(angles) * factor))

def reference(spatial_coeffs, temporal_basis, coil_maps, line_index, kspace_data):
    coeffs_wide = spatial_coeffs.astype(jnp.float32)
    maps_real = coil_maps[0].astype(jnp.float32)
    maps_imag = coil_maps[1].astype(jnp.float32)
    cosine, sine = dft_tables(NC)
    blocks = FRAMES // F_DEV
    basis_blocks = jnp.transpose(temporal_basis.reshape(L, blocks, F_DEV), (1, 0, 2))
    line_blocks = line_index.reshape(blocks, F_DEV, K)
    data_blocks = kspace_data.reshape(blocks, F_DEV, C, 2, K, NC)

    def frame_block(carry, block):
        basis_block, line_block, data_block = block
        basis_wide = basis_block.astype(jnp.float32)
        images = jnp.einsum('plrx,lt->tprx', coeffs_wide, basis_wide)
        img_real = images[:, 0][:, None]
        img_imag = images[:, 1][:, None]
        coil_real = keep_bf16(maps_real[None] * img_real - maps_imag[None] * img_imag)
        coil_imag = keep_bf16(maps_real[None] * img_imag + maps_imag[None] * img_real)
        hybrid_real = keep_bf16(jnp.einsum('tcrx,xk->tcrk', coil_real, cosine) - jnp.einsum('tcrx,xk->tcrk', coil_imag, sine))
        hybrid_imag = keep_bf16(jnp.einsum('tcrx,xk->tcrk', coil_real, sine) + jnp.einsum('tcrx,xk->tcrk', coil_imag, cosine))
        line_cos, line_sin = line_tables(line_block, NR)
        pred_real = jnp.einsum('tjr,tcrk->tcjk', line_cos, hybrid_real) - jnp.einsum('tjr,tcrk->tcjk', line_sin, hybrid_imag)
        pred_imag = jnp.einsum('tjr,tcrk->tcjk', line_cos, hybrid_imag) + jnp.einsum('tjr,tcrk->tcjk', line_sin, hybrid_real)
        data_wide = data_block.astype(jnp.float32)
        res_real = keep_bf16(pred_real - data_wide[:, :, 0])
        res_imag = keep_bf16(pred_imag - data_wide[:, :, 1])
        back_real = keep_bf16(jnp.einsum('tjr,tcjk->tcrk', line_cos, res_real) + jnp.einsum('tjr,tcjk->tcrk', line_sin, res_imag))
        back_imag = keep_bf16(jnp.einsum('tjr,tcjk->tcrk', line_cos, res_imag) - jnp.einsum('tjr,tcjk->tcrk', line_sin, res_real))
        adj_real = jnp.einsum('tcrk,xk->tcrx', back_real, cosine) + jnp.einsum('tcrk,xk->tcrx', back_imag, sine)
        adj_imag = jnp.einsum('tcrk,xk->tcrx', back_imag, cosine) - jnp.einsum('tcrk,xk->tcrx', back_real, sine)
        grad_real = lax.optimization_barrier(jnp.sum(maps_real[None] * adj_real + maps_imag[None] * adj_imag, axis=1))
        grad_imag = lax.optimization_barrier(jnp.sum(maps_real[None] * adj_imag - maps_imag[None] * adj_real, axis=1))
        frame_grad = keep_bf16(jnp.stack([grad_real, grad_imag], axis=1))
        carry = carry + jnp.einsum('tprx,lt->xplr', frame_grad, basis_wide)
        basis_part = jnp.einsum('plrx,tprx->lt', coeffs_wide, frame_grad) / NR
        return (carry, basis_part)
    start = jnp.zeros((NC, 2, L, NR), jnp.float32)
    coeff_grad, basis_parts = lax.scan(frame_block, start, (basis_blocks, line_blocks, data_blocks))
    basis_grad = jnp.transpose(basis_parts, (1, 0, 2)).reshape(L, FRAMES)
    return (coeff_grad, basis_grad)
```

```python
import math

import jax
import jax.numpy as jnp
import numpy as np
from jax import lax
from jax.experimental import pallas as pl
from jax.experimental.pallas import tpu as pltpu
from jax.sharding import PartitionSpec as P

F32 = jnp.float32
BF16 = jnp.bfloat16
VMEM = pl.BlockSpec(memory_space=pltpu.VMEM)
SMEM = pl.BlockSpec(memory_space=pltpu.SMEM)


def dot_nn(a, b):
    return lax.dot_general(a, b, (((1,), (0,)), ((), ())), preferred_element_type=F32)


def dot_nt(a, b, precision=None):
    return lax.dot_general(
        a, b, (((1,), (1,)), ((), ())), preferred_element_type=F32, precision=precision
    )


def dot_tn(a, b):
    return lax.dot_general(a, b, (((0,), (0,)), ((), ())), preferred_element_type=F32)


def iota(shape, axis):
    return lax.broadcasted_iota(jnp.int32, shape, axis)


def one_hot(condition):
    return jnp.where(condition, 1.0, 0.0).astype(BF16)


def dft_block(length):
    indices = np.arange(length, dtype=np.int64)
    phases = (indices[:, None] * indices[None, :]) % length
    angles = phases.astype(np.float32) * np.float32(2.0 * math.pi / length)
    factor = np.float32(1.0 / math.sqrt(length))
    cosine = np.cos(angles) * factor
    sine = -np.sin(angles) * factor
    top = np.concatenate([cosine, -sine], axis=1)
    low = np.concatenate([sine, cosine], axis=1)
    return np.concatenate([top, low], axis=0).astype(BF16)


def line_blocks(base, frames):
    lane_frame = iota(base.shape, 1) // (base.shape[1] // frames)
    wide = base.astype(F32)
    return jnp.concatenate(
        [jnp.where(lane_frame == t, wide, 0.0).astype(BF16) for t in range(frames)], axis=0
    )


def over_frames(block, frames):
    return jnp.concatenate([block] * frames, axis=0)


def forward_kernel(u_ref, phi_ref, maps_ref, base_a_ref, base_b_ref, dft_ref, out_ref):
    rank, frames = phi_ref.shape[1], phi_ref.shape[0]
    coils, rows, cols = maps_ref.shape[1:]
    lines = base_a_ref.shape[1]
    spread = one_hot(iota((rank, rank * rows), 1) // rows == iota((rank, rank * rows), 0))
    phi_wide = dot_nn(phi_ref[...], spread)
    same_row = iota((rows, rank * rows), 1) % rows == iota((rows, rank * rows), 0)
    mix = jnp.concatenate(
        [
            jnp.where(same_row, jnp.broadcast_to(phi_wide[t : t + 1], same_row.shape), 0.0).astype(BF16)
            for t in range(frames)
        ],
        axis=0,
    )
    img_real = dot_nn(mix, u_ref[0])
    img_imag = dot_nn(mix, u_ref[1])
    sampling = jnp.concatenate(
        [line_blocks(base_a_ref[...], frames), line_blocks(base_b_ref[...], frames)], axis=0
    )
    for c in range(coils):
        map_real = over_frames(maps_ref[0, c].astype(F32), frames)
        map_imag = over_frames(maps_ref[1, c].astype(F32), frames)
        coil_real = (map_real * img_real - map_imag * img_imag).astype(BF16)
        coil_imag = (map_real * img_imag + map_imag * img_real).astype(BF16)
        coil = jnp.concatenate([coil_real, coil_imag], axis=1)
        hybrid = dot_nt(dft_ref[...], coil).astype(BF16)
        hybrid = jnp.concatenate([hybrid[:cols], hybrid[cols:]], axis=1)
        out_ref[:, c * lines : (c + 1) * lines] = dot_nn(hybrid, sampling).astype(BF16)


def residual_kernel(parts_ref, data_ref, out_ref):
    members, span, width = parts_ref.shape
    total = parts_ref[0].astype(F32)
    for m in range(1, members):
        total = total + parts_ref[m].astype(F32)
    frames, coils, group = data_ref.shape[0], data_ref.shape[1], data_ref.shape[2]
    data = jnp.concatenate(
        [data_ref[t, c] for c in range(coils) for t in range(frames)], axis=0
    )
    eye = one_hot(iota((span, span), 0) == iota((span, span), 1))
    residual = (total - dot_nt(eye, data)).astype(BF16)
    for m in range(members):
        out_ref[m] = residual


def backward_kernel(
    with_phi, offset_ref, res_ref, u_ref, phi_ref, maps_ref, base_a_ref, base_b_ref, dft_ref,
    out_ref, basis_ref,
):
    rank, frames = phi_ref.shape[1], phi_ref.shape[0]
    coils, rows, cols = maps_ref.shape[1:]
    lines = base_a_ref.shape[1]
    half = cols // 2
    offset = pl.multiple_of(offset_ref[0], half)
    here = pl.ds(offset, half)
    there = pl.ds(pl.multiple_of(offset + cols, half), half)
    points = frames * rows
    sampling = jnp.concatenate(
        [line_blocks(base_a_ref[...], frames), line_blocks(base_b_ref[...], frames)], axis=0
    )
    adjoint = jnp.concatenate([dft_ref[:, here], dft_ref[:, there]], axis=1)
    grad_real = jnp.zeros((points, half), F32)
    grad_imag = jnp.zeros((points, half), F32)
    for c in range(coils):
        back = dot_nt(sampling, res_ref[:, c * lines : (c + 1) * lines]).astype(BF16)
        back = jnp.concatenate([back[:points], back[points:]], axis=1)
        adj = dot_nn(back, adjoint)
        adj_real, adj_imag = adj[:, :half], adj[:, half:]
        map_real = over_frames(maps_ref[0, c, :, here].astype(F32), frames)
        map_imag = over_frames(maps_ref[1, c, :, here].astype(F32), frames)
        grad_real = grad_real + (map_real * adj_real + map_imag * adj_imag)
        grad_imag = grad_imag + (map_real * adj_imag - map_imag * adj_real)
    grad_real = grad_real.astype(BF16)
    grad_imag = grad_imag.astype(BF16)
    quads = frames // 2
    places = half * quads
    moved = jnp.zeros((places, 2 * 2 * rows), F32)
    for q in range(quads):
        piece = jnp.concatenate(
            [grad_real[q * 2 * rows : (q + 1) * 2 * rows], grad_imag[q * 2 * rows : (q + 1) * 2 * rows]],
            axis=0,
        )
        chosen = one_hot(iota((places, half), 0) == iota((places, half), 1) * quads + q)
        moved = moved + dot_nt(chosen, piece)
    owners = out_ref.shape[0]
    size = places // owners
    out_ref[:, :size, :] = moved.astype(BF16).reshape(owners, size, 4 * rows)
    if with_phi:
        lanes = 4 * rank
        row, lane = iota((frames, lanes), 0), iota((frames, lanes), 1)
        spread = one_hot(iota((rank, lanes), 1) % rank == iota((rank, lanes), 0))
        phi_wide = dot_nn(phi_ref[...], spread).astype(BF16)
        square = (frames, frames)
        first = dot_nn(one_hot(iota(square, 1) == iota(square, 0) % quads * 2), phi_wide)
        second = dot_nn(one_hot(iota(square, 1) == iota(square, 0) % quads * 2 + 1), phi_wide)
        tile = jnp.where(lane // rank % 2 == 0, first, second)
        tile = jnp.where(lane // (2 * rank) == row // quads, tile, 0.0).astype(BF16)
        for d in range(owners):
            out_ref[d, size:, :] = tile
    both = jnp.concatenate([grad_real, grad_imag], axis=1)
    coeffs = jnp.concatenate([u_ref[0, :, here], u_ref[1, :, here]], axis=1)
    cross = dot_nt(coeffs, both)
    cross = cross.reshape(rank, rows, points)
    keep = iota((rows, points), 1) % rows == iota((rows, points), 0)
    per_rank = jnp.concatenate(
        [
            jnp.sum(jnp.where(keep, cross[l], 0.0), axis=0, keepdims=True)
            for l in range(rank)
        ],
        axis=0,
    )
    frame_sum = jnp.where(
        iota((frames, points), 1) // rows == iota((frames, points), 0), 1.0, 0.0
    )
    basis_ref[...] = dot_nt(frame_sum, per_rank, lax.Precision.HIGHEST)


def combine(parts, weights, rank):
    summed = []
    for h in range(2):
        part = parts[h]
        product = dot_tn(weights, part)
        halves = []
        for x in range(2):
            first = product[(2 * x) * rank : (2 * x + 1) * rank]
            second = product[(2 * x + 1) * rank : (2 * x + 2) * rank]
            halves.append(first + pltpu.roll(second, first.shape[1] - rank, 1))
        summed.append(jnp.concatenate(halves, axis=0))
    lane = iota(summed[0].shape, 1)
    return jnp.where(lane // rank % 2 == 0, summed[0], pltpu.roll(summed[1], rank, 1))


def tiles(ref, first):
    owners, lanes = ref.shape[0], ref.shape[2]
    wide = ref[:, first : first + 8, :].astype(F32)
    return wide.reshape(owners * 8, lanes).astype(BF16)


def far_kernel(a_ref, out_ref):
    rank = 32
    total = combine([tiles(a_ref, 0), tiles(a_ref, 8)], tiles(a_ref, 16), rank)
    out_ref[...] = total.astype(BF16)


def near_kernel(b_ref, a_ref, far_ref, out_ref):
    rank = out_ref.shape[2]
    rows = out_ref.shape[3]
    total = combine([tiles(b_ref, 0), tiles(b_ref, 8)], tiles(a_ref, 16), rank)
    total = total + far_ref[...].astype(F32)
    for h in range(2):
        for x in range(2):
            for p in range(2):
                lane = p * 2 * rows + h * rows
                out_ref[h * 2 + x, p] = total[x * rank : (x + 1) * rank, lane : lane + rows]


def call(kernel, out_shape, specs, flops, bytes_accessed):
    return pl.pallas_call(
        kernel,
        out_shape=out_shape,
        in_specs=specs,
        out_specs=jax.tree.map(lambda _: VMEM, out_shape),
        compiler_params=pltpu.CompilerParams(vmem_limit_bytes=40 * 1024 * 1024),
        cost_estimate=pl.CostEstimate(
            flops=flops, bytes_accessed=bytes_accessed, transcendentals=0
        ),
    )


def shape(dims, dtype):
    return jax.ShapeDtypeStruct(dims, dtype)


def local(spatial_coeffs, temporal_basis, coil_maps, line_index, kspace_data):
    rank, rows, cols = spatial_coeffs.shape[1:]
    frames = temporal_basis.shape[1]
    coils = coil_maps.shape[1]
    lines = line_index.shape[1]
    members = lax.axis_size("vox")
    devices = lax.axis_size("frm")
    owners = devices // 2
    span = kspace_data.shape[4]
    height = rows * members
    lanes = frames * 2 * lines

    dft = jnp.asarray(dft_block(cols))
    u = spatial_coeffs.reshape(2, rank * rows, cols)
    phi = temporal_basis.T
    row_numbers = lax.axis_index("vox") * rows + jnp.arange(rows, dtype=jnp.int32)
    wide_lines = jnp.broadcast_to(line_index[:, None, :], (frames, 2, lines)).reshape(1, lanes)
    phases = wide_lines * row_numbers[:, None] % height
    angles = phases.astype(F32) * (2.0 * math.pi / height)
    factor = 1.0 / math.sqrt(height)
    cosine = jnp.cos(angles) * factor
    sine = -jnp.sin(angles) * factor
    is_real = (jnp.arange(lanes, dtype=jnp.int32) // lines % 2 == 0)[None, :]
    base_a = jnp.where(is_real, cosine, sine).astype(BF16)
    base_b = jnp.where(is_real, -sine, cosine).astype(BF16)

    partial_lines = call(
        forward_kernel, shape((cols, coils * lanes), BF16), [VMEM] * 6, 2 * 10**9, 3 * 10**6
    )(u, phi, coil_maps, base_a, base_b, dft)
    parts = lax.all_to_all(
        partial_lines.reshape(members, span, coils * lanes), "vox", 0, 0, tiled=True
    )
    residual = call(
        residual_kernel, shape((members, span, coils * lanes), BF16), [VMEM] * 2, 10**7, 10**6
    )(parts, kspace_data.reshape(frames, coils, 2 * lines, span))
    residual = lax.all_to_all(residual, "vox", 0, 0, tiled=True)
    residual = residual.reshape(cols, coils * lanes)

    z_high = lax.axis_index("frm") // owners
    size = cols // 2 // owners * frames * 2 * rows // (4 * rows)

    def backward(offset, with_phi):
        depth = size + (frames if with_phi else 0)
        return call(
            lambda *refs: backward_kernel(with_phi, *refs),
            (shape((owners, depth, 4 * rows), BF16), shape((frames, rank), F32)),
            [SMEM] + [VMEM] * 7,
            2 * 10**9,
            3 * 10**6,
        )(offset.reshape(1), residual, u, phi, coil_maps, base_a, base_b, dft)

    groups = [list(range(owners)), list(range(owners, devices))]

    def exchange(chunks):
        return lax.all_to_all(chunks, "frm", 0, 0, tiled=True, axis_index_groups=groups)

    far_chunks, far_basis = backward((1 - z_high) * (cols // 2), True)
    far_chunks = exchange(far_chunks)
    near_chunks, near_basis = backward(z_high * (cols // 2), False)
    near_chunks = exchange(near_chunks)
    basis_term = far_basis + near_basis
    basis_all = lax.all_to_all(
        jnp.broadcast_to(basis_term[None], (members, frames, rank)), "vox", 0, 0, tiled=True
    )
    far = call(far_kernel, shape((2 * rank, 4 * rows), BF16), [VMEM], 10**7, 10**6)(far_chunks)
    far = lax.ppermute(far, "frm", [(i, (i + owners) % devices) for i in range(devices)])
    coeff_grad = call(
        near_kernel,
        shape((cols // devices, 2, rank, rows), F32),
        [VMEM] * 3,
        10**7,
        10**6,
    )(near_chunks, far_chunks, far)
    basis_grad = (jnp.sum(basis_all, axis=0) / height).T
    return (coeff_grad, basis_grad)


def solution(mesh):
    placed = (
        P(None, None, "vox", None),
        P(None, "frm"),
        P(None, None, "vox", None),
        P("frm", None),
        P("frm", None, None, None, "vox"),
    )
    return jax.shard_map(
        local,
        mesh=mesh,
        in_specs=placed,
        out_specs=(P("frm", None, None, "vox"), P(None, "frm")),
        check_vma=False,
    )
```

```python
import functools
import math

import jax
import jax.numpy as jnp
import numpy as np
from jax import lax
from jax.experimental import pallas as pl
from jax.experimental.pallas import tpu as pltpu
from jax.sharding import PartitionSpec as P

F32 = jnp.float32
BF16 = jnp.bfloat16
VMEM = pl.BlockSpec(memory_space=pltpu.VMEM)
SMEM = pl.BlockSpec(memory_space=pltpu.SMEM)
HBM = pl.BlockSpec(memory_space=pltpu.HBM)


def dot_nn(a, b):
    return lax.dot_general(a, b, (((1,), (0,)), ((), ())), preferred_element_type=F32)


def dot_nt(a, b, precision=None):
    return lax.dot_general(
        a, b, (((1,), (1,)), ((), ())), preferred_element_type=F32, precision=precision
    )


def dot_tn(a, b, precision=None):
    return lax.dot_general(
        a, b, (((0,), (0,)), ((), ())), preferred_element_type=F32, precision=precision
    )


def iota(shape, axis):
    return lax.broadcasted_iota(jnp.int32, shape, axis)


def one_hot(condition):
    return jnp.where(condition, 1.0, 0.0).astype(BF16)


def dft_block(length):
    indices = np.arange(length, dtype=np.int64)
    phases = (indices[:, None] * indices[None, :]) % length
    angles = phases.astype(np.float32) * np.float32(2.0 * math.pi / length)
    factor = np.float32(1.0 / math.sqrt(length))
    cosine = np.cos(angles) * factor
    sine = -np.sin(angles) * factor
    top = np.concatenate([cosine, -sine], axis=1)
    low = np.concatenate([sine, cosine], axis=1)
    return np.concatenate([top, low], axis=0).astype(BF16)


def line_blocks(base, frames):
    lane_frame = iota(base.shape, 1) // (base.shape[1] // frames)
    wide = base.astype(F32)
    return jnp.concatenate(
        [jnp.where(lane_frame == t, wide, 0.0).astype(BF16) for t in range(frames)], axis=0
    )


def over_frames(block, frames):
    return jnp.concatenate([block] * frames, axis=0)


def line_tables(v, lines_ref, dft_ref, rows, frames):
    cols = dft_ref.shape[0] // 2
    count = lines_ref.shape[1]
    lanes = frames * 2 * count
    spread = one_hot(iota((count, lanes), 1) % count == iota((count, lanes), 0))
    wide = dot_nn(lines_ref[...].astype(F32).astype(BF16), spread)
    mine = iota((frames, lanes), 1) // (2 * count) == iota((frames, lanes), 0)
    number = jnp.sum(jnp.where(mine, wide, 0.0), axis=0, keepdims=True).astype(jnp.int32)
    chosen = one_hot(iota((cols, lanes), 0) == number)
    first = pl.multiple_of(v * rows, rows)
    cosine = dot_nn(dft_ref[pl.ds(first, rows), :cols], chosen)
    sine = dot_nn(dft_ref[pl.ds(pl.multiple_of(cols + first, rows), rows), :cols], chosen)
    is_real = iota((rows, lanes), 1) // count % 2 == 0
    return jnp.where(is_real, cosine, sine), jnp.where(is_real, -sine, cosine)


def basis_tile(phi_ref):
    rank, frames = phi_ref.shape[1], phi_ref.shape[0]
    quads = frames // 2
    lanes = 4 * rank
    row, lane = iota((frames, lanes), 0), iota((frames, lanes), 1)
    spread = one_hot(iota((rank, lanes), 1) % rank == iota((rank, lanes), 0))
    phi_wide = dot_nn(phi_ref[...], spread).astype(BF16)
    square = (frames, frames)
    first = dot_nn(one_hot(iota(square, 1) == iota(square, 0) % quads * 2), phi_wide)
    second = dot_nn(one_hot(iota(square, 1) == iota(square, 0) % quads * 2 + 1), phi_wide)
    tile = jnp.where(lane // rank % 2 == 0, first, second)
    return jnp.where(lane // (2 * rank) == row // quads, tile, 0.0)


def forward_kernel(
    v_ref, u_hbm, phi_hbm, maps_hbm, lines_hbm, dft_hbm, out_ref, tables_ref,
    u_ref, phi_ref, maps_ref, lines_ref, dft_ref, sems,
):
    copies = [
        pltpu.make_async_copy(source, target, sems.at[i])
        for i, (source, target) in enumerate(
            [
                (phi_hbm, phi_ref),
                (lines_hbm, lines_ref),
                (dft_hbm, dft_ref),
                (u_hbm, u_ref),
                (maps_hbm, maps_ref),
            ]
        )
    ]
    for copy in copies:
        copy.start()
    rank, frames = phi_ref.shape[1], phi_ref.shape[0]
    coils, rows, cols = maps_ref.shape[1:]
    spread = one_hot(iota((rank, rank * rows), 1) // rows == iota((rank, rank * rows), 0))
    same_row = iota((rows, rank * rows), 1) % rows == iota((rows, rank * rows), 0)
    copies[0].wait()
    phi_wide = dot_nn(phi_ref[...], spread)
    mix = jnp.concatenate(
        [
            jnp.where(same_row, jnp.broadcast_to(phi_wide[t : t + 1], same_row.shape), 0.0).astype(BF16)
            for t in range(frames)
        ],
        axis=0,
    )
    copies[1].wait()
    copies[2].wait()
    base_a, base_b = line_tables(v_ref[0], lines_ref, dft_ref, rows, frames)
    lines = base_a.shape[1]
    tables = [base_a, base_b, basis_tile(phi_ref)]
    tables.append(jnp.zeros((tables_ref.shape[0] - sum(t.shape[0] for t in tables), lines), F32))
    tables_ref[...] = jnp.concatenate(tables, axis=0).astype(BF16)
    sampling = jnp.concatenate(
        [line_blocks(base_a.astype(BF16), frames), line_blocks(base_b.astype(BF16), frames)], axis=0
    )
    quad, span = out_ref.shape[0], out_ref.shape[1] // 2
    copies[3].wait()
    copies[4].wait()
    img_real = dot_nn(mix, u_ref[0])
    img_imag = dot_nn(mix, u_ref[1])
    for c in range(coils):
        map_real = over_frames(maps_ref[0, c].astype(F32), frames)
        map_imag = over_frames(maps_ref[1, c].astype(F32), frames)
        coil_real = (map_real * img_real - map_imag * img_imag).astype(BF16)
        coil_imag = (map_real * img_imag + map_imag * img_real).astype(BF16)
        coil = jnp.concatenate([coil_real, coil_imag], axis=1)
        hybrid = dot_nt(dft_ref[...], coil).astype(BF16)
        hybrid = jnp.concatenate([hybrid[:cols], hybrid[cols:]], axis=1)
        found = dot_nn(hybrid, sampling).astype(BF16)
        for b in range(2 * quad):
            out_ref[b % quad, b // quad * span : (b // quad + 1) * span, c * lines : (c + 1) * lines] = (
                found[b * span : (b + 1) * span]
            )


def quad_kernel(half_ref, parts_ref, data_ref, out_ref):
    total = parts_ref[0].astype(F32)
    for m in range(1, parts_ref.shape[0]):
        total = total + parts_ref[m].astype(F32)
    frames, coils, _, span = data_ref.shape
    data = jnp.concatenate(
        [data_ref[t, c] for c in range(coils) for t in range(frames)], axis=0
    )
    eye = one_hot(iota((span, span), 0) == iota((span, span), 1))
    measured = dot_nt(eye, data)
    for h in range(2):
        rows = slice(h * span, (h + 1) * span)
        out_ref[rows, :] = (total[rows] - jnp.where(half_ref[0] == h, measured, 0.0)).astype(BF16)


def residual_kernel(mine_ref, other_ref, out_ref):
    residual = (mine_ref[...].astype(F32) + other_ref[...].astype(F32)).astype(BF16)
    for m in range(out_ref.shape[0]):
        out_ref[m] = residual


def backward_kernel(
    res_ref, u_ref, maps_ref, tables_ref, dft_ref, out_ref, basis_ref
):
    coils, rows, cols = maps_ref.shape[1:]
    frames, rank = basis_ref.shape[0], u_ref.shape[1] // rows
    lines = tables_ref.shape[1]
    quad, span = res_ref.shape[0], res_ref.shape[1] // 2
    points = frames * rows
    sampling = jnp.concatenate(
        [line_blocks(tables_ref[i * rows : (i + 1) * rows, :], frames) for i in range(2)], axis=0
    )
    grad_real = jnp.zeros((points, cols), F32)
    grad_imag = jnp.zeros((points, cols), F32)
    for c in range(coils):
        found = jnp.concatenate(
            [
                res_ref[b % quad, b // quad * span : (b // quad + 1) * span, c * lines : (c + 1) * lines]
                for b in range(2 * quad)
            ],
            axis=0,
        )
        back = dot_nt(sampling, found).astype(BF16)
        back = jnp.concatenate([back[:points], back[points:]], axis=1)
        adj = dot_nn(back, dft_ref[...])
        adj_real, adj_imag = adj[:, :cols], adj[:, cols:]
        map_real = over_frames(maps_ref[0, c].astype(F32), frames)
        map_imag = over_frames(maps_ref[1, c].astype(F32), frames)
        grad_real = grad_real + (map_real * adj_real + map_imag * adj_imag)
        grad_imag = grad_imag + (map_real * adj_imag - map_imag * adj_real)
    grad_real = grad_real.astype(BF16)
    grad_imag = grad_imag.astype(BF16)
    half = cols // 2
    quads = frames // 2
    places = half * quads
    owners = out_ref.shape[0]
    size = places // owners
    for z in range(2):
        moved = jnp.zeros((places, 4 * rows), F32)
        for q in range(quads):
            piece = jnp.concatenate(
                [
                    g[q * 2 * rows : (q + 1) * 2 * rows, z * half : (z + 1) * half]
                    for g in (grad_real, grad_imag)
                ],
                axis=0,
            )
            chosen = one_hot(iota((places, half), 0) == iota((places, half), 1) * quads + q)
            moved = moved + dot_nt(chosen, piece)
        out_ref[:, z * size : (z + 1) * size, :] = moved.astype(BF16).reshape(
            owners, size, 4 * rows
        )
    tile = tables_ref[2 * rows : 2 * rows + frames, :]
    for d in range(owners):
        out_ref[d, 2 * size :, :] = tile
    both = jnp.concatenate([grad_real, grad_imag], axis=1)
    coeffs = jnp.concatenate([u_ref[0], u_ref[1]], axis=1)
    cross = dot_nt(coeffs, both).reshape(rank, rows, points)
    keep = iota((rows, points), 1) % rows == iota((rows, points), 0)
    per_rank = jnp.concatenate(
        [
            jnp.sum(jnp.where(keep, cross[l], 0.0), axis=0, keepdims=True)
            for l in range(rank)
        ],
        axis=0,
    )
    frame_sum = jnp.where(
        iota((frames, points), 1) // rows == iota((frames, points), 0), 1.0, 0.0
    )
    per_rank = jnp.concatenate(
        [per_rank, jnp.zeros((basis_ref.shape[1] - rank, points), F32)], axis=0
    )
    basis_ref[...] = dot_nt(frame_sum, per_rank, lax.Precision.HIGHEST)


def tiles(ref, first):
    owners, lanes = ref.shape[0], ref.shape[2]
    wide = ref[:, pl.ds(first, 8), :].astype(F32)
    return wide.reshape(owners * 8, lanes).astype(BF16)


def combine(ref, first, rank):
    weights = tiles(ref, 32)
    summed = []
    for h in range(2):
        product = dot_tn(weights, tiles(ref, pl.multiple_of(first + 8 * h, 8)))
        halves = []
        for x in range(2):
            even = product[(2 * x) * rank : (2 * x + 1) * rank]
            odd = product[(2 * x + 1) * rank : (2 * x + 2) * rank]
            halves.append(even + pltpu.roll(odd, odd.shape[1] - rank, 1))
        summed.append(jnp.concatenate(halves, axis=0))
    lane = iota(summed[0].shape, 1)
    return jnp.where(lane // rank % 2 == 0, summed[0], pltpu.roll(summed[1], rank, 1))


def contract_kernel(z_ref, chunks_ref, far_ref, near_ref):
    rank = far_ref.shape[0] // 2
    z = z_ref[0]
    far_ref[...] = combine(chunks_ref, (1 - z) * 16, rank).astype(BF16)
    near_ref[...] = combine(chunks_ref, z * 16, rank)


def sum_kernel(*refs):
    total = refs[0][...]
    for ref in refs[1:-1]:
        total = total + ref[...]
    out_ref = refs[-1]
    if len(out_ref.shape) == len(total.shape):
        out_ref[...] = total
    else:
        for m in range(out_ref.shape[0]):
            out_ref[m] = total


def finish_kernel(height, near_ref, far_ref, basis_ref, out_ref, basis_out_ref):
    rank, rows = out_ref.shape[2:]
    total = near_ref[...] + far_ref[...].astype(F32)
    for h in range(2):
        for x in range(2):
            for p in range(2):
                lane = p * 2 * rows + h * rows
                out_ref[h * 2 + x, p] = total[x * rank : (x + 1) * rank, lane : lane + rows]
    basis = sum(basis_ref[m] for m in range(basis_ref.shape[0])) / height
    basis_out_ref[...] = basis[:, :rank]


def call(kernel, out_shape, specs, flops, bytes_accessed, scratch=(), vmem_mib=40):
    return pl.pallas_call(
        kernel,
        out_shape=out_shape,
        in_specs=specs,
        out_specs=jax.tree.map(lambda _: VMEM, out_shape),
        scratch_shapes=scratch,
        compiler_params=pltpu.CompilerParams(vmem_limit_bytes=vmem_mib * 2**20),
        cost_estimate=pl.CostEstimate(
            flops=flops, bytes_accessed=bytes_accessed, transcendentals=0
        ),
    )


def shape(dims, dtype):
    return jax.ShapeDtypeStruct(dims, dtype)


def swapped(count, step):
    return [(i, i ^ step) for i in range(count)]


def steps(spatial_coeffs, temporal_basis, coil_maps, line_index, kspace_data):
    rank, rows, cols = spatial_coeffs.shape[1:]
    frames = temporal_basis.shape[1]
    coils = coil_maps.shape[1]
    lines = line_index.shape[1]
    members = lax.axis_size("vox")
    devices = lax.axis_size("frm")
    owners = devices // 2
    span = kspace_data.shape[4]
    quad = members // 2
    quads = [list(range(quad)), list(range(quad, members))]
    height = rows * members
    lanes = frames * 2 * lines

    dft = jnp.asarray(dft_block(cols))
    u = spatial_coeffs.reshape(2, rank * rows, cols)
    phi = temporal_basis.T
    partial_lines, tables = call(
        forward_kernel,
        (shape((quad, 2 * span, coils * lanes), BF16), shape((2 * rows + 16, lanes), BF16)),
        [SMEM] + [HBM] * 5,
        2 * 10**9,
        3 * 10**6,
        scratch=[
            pltpu.VMEM(u.shape, BF16),
            pltpu.VMEM(phi.shape, BF16),
            pltpu.VMEM(coil_maps.shape, BF16),
            pltpu.VMEM(line_index.shape, jnp.int32),
            pltpu.VMEM(dft.shape, BF16),
            pltpu.SemaphoreType.DMA((5,)),
        ],
        vmem_mib=63,
    )(lax.axis_index("vox").reshape(1), u, phi, coil_maps, line_index, dft)
    parts = lax.all_to_all(partial_lines, "vox", 0, 0, tiled=True, axis_index_groups=quads)
    block = (2 * span, coils * lanes)
    mine = call(quad_kernel, shape(block, BF16), [SMEM] + [VMEM] * 2, 10**7, 10**6)(
        (lax.axis_index("vox") // quad).reshape(1),
        parts,
        kspace_data.reshape(frames, coils, 2 * lines, span),
    )
    other = lax.ppermute(mine, "vox", swapped(members, quad))
    residual = call(residual_kernel, shape((quad, *block), BF16), [VMEM] * 2, 10**7, 10**6)(
        mine, other
    )
    residual = lax.all_to_all(residual, "vox", 0, 0, tiled=True, axis_index_groups=quads)

    z_high = lax.axis_index("frm") // owners
    depth = cols // devices * 2 * frames // 2 + frames
    chunks, basis_term = call(
        backward_kernel,
        (shape((owners, depth, 4 * rows), BF16), shape((frames, lanes), F32)),
        [VMEM] * 5,
        4 * 10**9,
        3 * 10**6,
    )(residual, u, coil_maps, tables, dft)
    groups = [list(range(owners)), list(range(owners, devices))]
    chunks = lax.all_to_all(chunks, "frm", 0, 0, tiled=True, axis_index_groups=groups)
    basis_part = lax.ppermute(basis_term, "vox", swapped(members, quad))
    basis_term = call(
        sum_kernel, shape((quad, frames, lanes), F32), [VMEM] * 2, 10**4, 10**4
    )(basis_term, basis_part)
    far, near = call(
        contract_kernel,
        (shape((2 * rank, 4 * rows), BF16), shape((2 * rank, 4 * rows), F32)),
        [SMEM, VMEM],
        10**7,
        10**6,
    )(z_high.reshape(1), chunks)
    far = lax.ppermute(far, "frm", swapped(devices, owners))
    basis_all = lax.all_to_all(
        basis_term, "vox", 0, 0, tiled=True,
        axis_index_groups=quads,
    )
    coeff_grad, basis_grad = call(
        functools.partial(finish_kernel, height),
        (shape((cols // devices, 2, rank, rows), F32), shape((frames, rank), F32)),
        [VMEM] * 3,
        10**6,
        10**6,
    )(near, far, basis_all)
    return (coeff_grad, basis_grad.T)


def solution(mesh):
    placed = (
        P(None, None, "vox", None),
        P(None, "frm"),
        P(None, None, "vox", None),
        P("frm", None),
        P("frm", None, None, None, "vox"),
    )
    return jax.shard_map(
        steps,
        mesh=mesh,
        in_specs=placed,
        out_specs=(P("frm", None, None, "vox"), P(None, "frm")),
        check_vma=False,
    )
```

```python
import functools
import math

import jax
import jax.numpy as jnp
import numpy as np
from jax import lax
from jax.experimental import pallas as pl
from jax.experimental.pallas import tpu as pltpu
from jax.sharding import PartitionSpec as P

F32 = jnp.float32
BF16 = jnp.bfloat16
VMEM = pl.BlockSpec(memory_space=pltpu.VMEM)
SMEM = pl.BlockSpec(memory_space=pltpu.SMEM)
HBM = pl.BlockSpec(memory_space=pltpu.HBM)


def dot_nn(a, b):
    return lax.dot_general(a, b, (((1,), (0,)), ((), ())), preferred_element_type=F32)


def dot_nt(a, b, precision=None):
    return lax.dot_general(
        a, b, (((1,), (1,)), ((), ())), preferred_element_type=F32, precision=precision
    )


def dot_tn(a, b, precision=None):
    return lax.dot_general(
        a, b, (((0,), (0,)), ((), ())), preferred_element_type=F32, precision=precision
    )


def iota(shape, axis):
    return lax.broadcasted_iota(jnp.int32, shape, axis)


def one_hot(condition):
    return jnp.where(condition, 1.0, 0.0).astype(BF16)


def dft_block(length):
    indices = np.arange(length, dtype=np.int64)
    phases = (indices[:, None] * indices[None, :]) % length
    angles = phases.astype(np.float32) * np.float32(2.0 * math.pi / length)
    factor = np.float32(1.0 / math.sqrt(length))
    cosine = np.cos(angles) * factor
    sine = -np.sin(angles) * factor
    top = np.concatenate([cosine, -sine], axis=1)
    low = np.concatenate([sine, cosine], axis=1)
    return np.concatenate([top, low], axis=0).astype(BF16)


def line_blocks(base, frames):
    lane_frame = iota(base.shape, 1) // (base.shape[1] // frames)
    wide = base.astype(F32)
    return jnp.concatenate(
        [jnp.where(lane_frame == t, wide, 0.0).astype(BF16) for t in range(frames)], axis=0
    )


def over_frames(block, frames):
    return jnp.concatenate([block] * frames, axis=0)


def line_tables(v, lines_ref, dft_ref, rows, frames):
    cols = dft_ref.shape[0] // 2
    count = lines_ref.shape[1]
    lanes = frames * 2 * count
    spread = one_hot(iota((count, lanes), 1) % count == iota((count, lanes), 0))
    wide = dot_nn(lines_ref[...].astype(F32).astype(BF16), spread)
    mine = iota((frames, lanes), 1) // (2 * count) == iota((frames, lanes), 0)
    number = jnp.sum(jnp.where(mine, wide, 0.0), axis=0, keepdims=True).astype(jnp.int32)
    chosen = one_hot(iota((cols, lanes), 0) == number)
    first = pl.multiple_of(v * rows, rows)
    cosine = dot_nn(dft_ref[pl.ds(first, rows), :cols], chosen)
    sine = dot_nn(dft_ref[pl.ds(pl.multiple_of(cols + first, rows), rows), :cols], chosen)
    is_real = iota((rows, lanes), 1) // count % 2 == 0
    return jnp.where(is_real, cosine, sine), jnp.where(is_real, -sine, cosine)


def basis_tile(phi_ref):
    rank, frames = phi_ref.shape[1], phi_ref.shape[0]
    quads = frames // 2
    lanes = 4 * rank
    row, lane = iota((frames, lanes), 0), iota((frames, lanes), 1)
    spread = one_hot(iota((rank, lanes), 1) % rank == iota((rank, lanes), 0))
    phi_wide = dot_nn(phi_ref[...], spread).astype(BF16)
    square = (frames, frames)
    first = dot_nn(one_hot(iota(square, 1) == iota(square, 0) % quads * 2), phi_wide)
    second = dot_nn(one_hot(iota(square, 1) == iota(square, 0) % quads * 2 + 1), phi_wide)
    tile = jnp.where(lane // rank % 2 == 0, first, second)
    return jnp.where(lane // (2 * rank) == row // quads, tile, 0.0)


def forward_kernel(
    v_ref, u_hbm, phi_hbm, maps_hbm, lines_hbm, dft_hbm, out_ref, tables_ref,
    u_ref, phi_ref, maps_ref, lines_ref, dft_ref, sems,
):
    copies = [
        pltpu.make_async_copy(source, target, sems.at[i])
        for i, (source, target) in enumerate(
            [
                (phi_hbm, phi_ref),
                (lines_hbm, lines_ref),
                (dft_hbm, dft_ref),
                (u_hbm, u_ref),
                (maps_hbm, maps_ref),
            ]
        )
    ]
    for copy in copies:
        copy.start()
    rank, frames = phi_ref.shape[1], phi_ref.shape[0]
    coils, rows, cols = maps_ref.shape[1:]
    spread = one_hot(iota((rank, rank * rows), 1) // rows == iota((rank, rank * rows), 0))
    same_row = iota((rows, rank * rows), 1) % rows == iota((rows, rank * rows), 0)
    copies[0].wait()
    phi_wide = dot_nn(phi_ref[...], spread)
    mix = jnp.concatenate(
        [
            jnp.where(same_row, jnp.broadcast_to(phi_wide[t : t + 1], same_row.shape), 0.0).astype(BF16)
            for t in range(frames)
        ],
        axis=0,
    )
    copies[1].wait()
    copies[2].wait()
    base_a, base_b = line_tables(v_ref[0], lines_ref, dft_ref, rows, frames)
    lines = base_a.shape[1]
    tables = [base_a, base_b, basis_tile(phi_ref)]
    tables.append(jnp.zeros((tables_ref.shape[0] - sum(t.shape[0] for t in tables), lines), F32))
    tables_ref[...] = jnp.concatenate(tables, axis=0).astype(BF16)
    sampling = jnp.concatenate(
        [line_blocks(base_a.astype(BF16), frames), line_blocks(base_b.astype(BF16), frames)], axis=0
    )
    quad, span = out_ref.shape[0], out_ref.shape[1] // 2
    copies[3].wait()
    copies[4].wait()
    img_real = dot_nn(mix, u_ref[0])
    img_imag = dot_nn(mix, u_ref[1])
    for c in range(coils):
        map_real = over_frames(maps_ref[0, c].astype(F32), frames)
        map_imag = over_frames(maps_ref[1, c].astype(F32), frames)
        coil_real = (map_real * img_real - map_imag * img_imag).astype(BF16)
        coil_imag = (map_real * img_imag + map_imag * img_real).astype(BF16)
        coil = jnp.concatenate([coil_real, coil_imag], axis=1)
        hybrid = dot_nt(dft_ref[...], coil).astype(BF16)
        hybrid = jnp.concatenate([hybrid[:cols], hybrid[cols:]], axis=1)
        found = dot_nn(hybrid, sampling).astype(BF16)
        for b in range(2 * quad):
            out_ref[b % quad, b // quad * span : (b // quad + 1) * span, c * lines : (c + 1) * lines] = (
                found[b * span : (b + 1) * span]
            )


def quad_kernel(half_ref, parts_ref, data_ref, out_ref):
    total = parts_ref[0].astype(F32)
    for m in range(1, parts_ref.shape[0]):
        total = total + parts_ref[m].astype(F32)
    frames, coils, _, span = data_ref.shape
    data = jnp.concatenate(
        [data_ref[t, c] for c in range(coils) for t in range(frames)], axis=0
    )
    eye = one_hot(iota((span, span), 0) == iota((span, span), 1))
    measured = dot_nt(eye, data)
    for h in range(2):
        rows = slice(h * span, (h + 1) * span)
        out_ref[rows, :] = (total[rows] - jnp.where(half_ref[0] == h, measured, 0.0)).astype(BF16)


def residual_kernel(mine_ref, other_ref, out_ref):
    residual = (mine_ref[...].astype(F32) + other_ref[...].astype(F32)).astype(BF16)
    for m in range(out_ref.shape[0]):
        out_ref[m] = residual


def backward_kernel(
    res_ref, u_ref, maps_ref, tables_ref, dft_ref, out_ref, basis_ref
):
    coils, rows, cols = maps_ref.shape[1:]
    frames, rank = basis_ref.shape[0], u_ref.shape[1] // rows
    lines = tables_ref.shape[1]
    quad, span = res_ref.shape[0], res_ref.shape[1] // 2
    points = frames * rows
    sampling = jnp.concatenate(
        [line_blocks(tables_ref[i * rows : (i + 1) * rows, :], frames) for i in range(2)], axis=0
    )
    grad_real = jnp.zeros((points, cols), F32)
    grad_imag = jnp.zeros((points, cols), F32)
    for c in range(coils):
        found = jnp.concatenate(
            [
                res_ref[b % quad, b // quad * span : (b // quad + 1) * span, c * lines : (c + 1) * lines]
                for b in range(2 * quad)
            ],
            axis=0,
        )
        back = dot_nt(sampling, found).astype(BF16)
        back = jnp.concatenate([back[:points], back[points:]], axis=1)
        adj = dot_nn(back, dft_ref[...])
        adj_real, adj_imag = adj[:, :cols], adj[:, cols:]
        map_real = over_frames(maps_ref[0, c].astype(F32), frames)
        map_imag = over_frames(maps_ref[1, c].astype(F32), frames)
        grad_real = grad_real + (map_real * adj_real + map_imag * adj_imag)
        grad_imag = grad_imag + (map_real * adj_imag - map_imag * adj_real)
    grad_real = grad_real.astype(BF16)
    grad_imag = grad_imag.astype(BF16)
    half = cols // 2
    quads = frames // 2
    places = half * quads
    owners = out_ref.shape[0]
    size = places // owners
    moved = jnp.zeros((places, 8 * rows), F32)
    for q in range(0, quads, 2):
        pieces = jnp.concatenate(
            [
                jnp.concatenate(
                    [
                        g[i * 2 * rows : (i + 1) * 2 * rows, z * half : (z + 1) * half]
                        for i in (q, q + 1)
                    ],
                    axis=1,
                )
                for z in range(2)
                for g in (grad_real, grad_imag)
            ],
            axis=0,
        )
        row, lane = iota((places, 2 * half), 0), iota((places, 2 * half), 1)
        chosen = one_hot(row == lane % half * quads + q + lane // half)
        moved = moved + dot_nt(chosen, pieces)
    moved = moved.astype(BF16)
    for z in range(2):
        out_ref[:, z * size : (z + 1) * size, :] = moved[:, z * 4 * rows : (z + 1) * 4 * rows].reshape(
            owners, size, 4 * rows
        )
    tile = tables_ref[2 * rows : 2 * rows + frames, :]
    for d in range(owners):
        out_ref[d, 2 * size :, :] = tile
    both = jnp.concatenate([grad_real, grad_imag], axis=1)
    coeffs = jnp.concatenate([u_ref[0], u_ref[1]], axis=1)
    cross = dot_nt(coeffs, both).reshape(rank, rows, points)
    keep = iota((rows, points), 1) % rows == iota((rows, points), 0)
    per_rank = jnp.concatenate(
        [
            jnp.sum(jnp.where(keep, cross[l], 0.0), axis=0, keepdims=True)
            for l in range(rank)
        ],
        axis=0,
    )
    frame_sum = jnp.where(
        iota((frames, points), 1) // rows == iota((frames, points), 0), 1.0, 0.0
    )
    per_rank = jnp.concatenate(
        [per_rank, jnp.zeros((basis_ref.shape[1] - rank, points), F32)], axis=0
    )
    basis_ref[...] = dot_nt(frame_sum, per_rank, lax.Precision.HIGHEST)


def tiles(ref, first):
    owners, lanes = ref.shape[0], ref.shape[2]
    wide = ref[:, pl.ds(first, 8), :].astype(F32)
    return wide.reshape(owners * 8, lanes).astype(BF16)


def combine(ref, first, rank):
    weights = tiles(ref, 32)
    summed = []
    for h in range(2):
        product = dot_tn(weights, tiles(ref, pl.multiple_of(first + 8 * h, 8)))
        halves = []
        for x in range(2):
            even = product[(2 * x) * rank : (2 * x + 1) * rank]
            odd = product[(2 * x + 1) * rank : (2 * x + 2) * rank]
            halves.append(even + pltpu.roll(odd, odd.shape[1] - rank, 1))
        summed.append(jnp.concatenate(halves, axis=0))
    lane = iota(summed[0].shape, 1)
    return jnp.where(lane // rank % 2 == 0, summed[0], pltpu.roll(summed[1], rank, 1))


def contract_kernel(z_ref, chunks_ref, far_ref, near_ref):
    rank = far_ref.shape[0] // 2
    z = z_ref[0]
    far_ref[...] = combine(chunks_ref, (1 - z) * 16, rank).astype(BF16)
    near_ref[...] = combine(chunks_ref, z * 16, rank)


def sum_kernel(*refs):
    total = refs[0][...]
    for ref in refs[1:-1]:
        total = total + ref[...]
    out_ref = refs[-1]
    if len(out_ref.shape) == len(total.shape):
        out_ref[...] = total
    else:
        for m in range(out_ref.shape[0]):
            out_ref[m] = total


def finish_kernel(height, near_ref, far_ref, basis_ref, out_ref, basis_out_ref):
    rank, rows = out_ref.shape[2:]
    total = near_ref[...] + far_ref[...].astype(F32)
    for h in range(2):
        for x in range(2):
            for p in range(2):
                lane = p * 2 * rows + h * rows
                out_ref[h * 2 + x, p] = total[x * rank : (x + 1) * rank, lane : lane + rows]
    basis = sum(basis_ref[m] for m in range(basis_ref.shape[0])) / height
    basis_out_ref[...] = basis[:, :rank]


def call(kernel, out_shape, specs, flops, bytes_accessed, scratch=(), vmem_mib=40):
    return pl.pallas_call(
        kernel,
        out_shape=out_shape,
        in_specs=specs,
        out_specs=jax.tree.map(lambda _: VMEM, out_shape),
        scratch_shapes=scratch,
        compiler_params=pltpu.CompilerParams(vmem_limit_bytes=vmem_mib * 2**20),
        cost_estimate=pl.CostEstimate(
            flops=flops, bytes_accessed=bytes_accessed, transcendentals=0
        ),
    )


def shape(dims, dtype):
    return jax.ShapeDtypeStruct(dims, dtype)


def swapped(count, step):
    return [(i, i ^ step) for i in range(count)]


def steps(spatial_coeffs, temporal_basis, coil_maps, line_index, kspace_data):
    rank, rows, cols = spatial_coeffs.shape[1:]
    frames = temporal_basis.shape[1]
    coils = coil_maps.shape[1]
    lines = line_index.shape[1]
    members = lax.axis_size("vox")
    devices = lax.axis_size("frm")
    owners = devices // 2
    span = kspace_data.shape[4]
    quad = members // 2
    quads = [list(range(quad)), list(range(quad, members))]
    height = rows * members
    lanes = frames * 2 * lines

    dft = jnp.asarray(dft_block(cols))
    u = spatial_coeffs.reshape(2, rank * rows, cols)
    phi = temporal_basis.T
    partial_lines, tables = call(
        forward_kernel,
        (shape((quad, 2 * span, coils * lanes), BF16), shape((2 * rows + 16, lanes), BF16)),
        [SMEM] + [HBM] * 5,
        2 * 10**9,
        3 * 10**6,
        scratch=[
            pltpu.VMEM(u.shape, BF16),
            pltpu.VMEM(phi.shape, BF16),
            pltpu.VMEM(coil_maps.shape, BF16),
            pltpu.VMEM(line_index.shape, jnp.int32),
            pltpu.VMEM(dft.shape, BF16),
            pltpu.SemaphoreType.DMA((5,)),
        ],
        vmem_mib=63,
    )(lax.axis_index("vox").reshape(1), u, phi, coil_maps, line_index, dft)
    parts = lax.all_to_all(partial_lines, "vox", 0, 0, tiled=True, axis_index_groups=quads)
    block = (2 * span, coils * lanes)
    mine = call(quad_kernel, shape(block, BF16), [SMEM] + [VMEM] * 2, 10**7, 10**6)(
        (lax.axis_index("vox") // quad).reshape(1),
        parts,
        kspace_data.reshape(frames, coils, 2 * lines, span),
    )
    other = lax.ppermute(mine, "vox", swapped(members, quad))
    residual = call(residual_kernel, shape((quad, *block), BF16), [VMEM] * 2, 10**7, 10**6)(
        mine, other
    )
    residual = lax.all_to_all(residual, "vox", 0, 0, tiled=True, axis_index_groups=quads)

    z_high = lax.axis_index("frm") // owners
    depth = cols // devices * 2 * frames // 2 + frames
    chunks, basis_term = call(
        backward_kernel,
        (shape((owners, depth, 4 * rows), BF16), shape((frames, lanes), F32)),
        [VMEM] * 5,
        4 * 10**9,
        3 * 10**6,
    )(residual, u, coil_maps, tables, dft)
    groups = [list(range(owners)), list(range(owners, devices))]
    chunks = lax.all_to_all(chunks, "frm", 0, 0, tiled=True, axis_index_groups=groups)
    basis_part = lax.ppermute(basis_term, "vox", swapped(members, quad))
    basis_term = call(
        sum_kernel, shape((quad, frames, lanes), F32), [VMEM] * 2, 10**4, 10**4
    )(basis_term, basis_part)
    far, near = call(
        contract_kernel,
        (shape((2 * rank, 4 * rows), BF16), shape((2 * rank, 4 * rows), F32)),
        [SMEM, VMEM],
        10**7,
        10**6,
    )(z_high.reshape(1), chunks)
    far = lax.ppermute(far, "frm", swapped(devices, owners))
    basis_all = lax.all_to_all(
        basis_term, "vox", 0, 0, tiled=True,
        axis_index_groups=quads,
    )
    coeff_grad, basis_grad = call(
        functools.partial(finish_kernel, height),
        (shape((cols // devices, 2, rank, rows), F32), shape((frames, rank), F32)),
        [VMEM] * 3,
        10**6,
        10**6,
    )(near, far, basis_all)
    return (coeff_grad, basis_grad.T)


def solution(mesh):
    placed = (
        P(None, None, "vox", None),
        P(None, "frm"),
        P(None, None, "vox", None),
        P("frm", None),
        P("frm", None, None, None, "vox"),
    )
    return jax.shard_map(
        steps,
        mesh=mesh,
        in_specs=placed,
        out_specs=(P("frm", None, None, "vox"), P(None, "frm")),
        check_vma=False,
    )
```
